32 devices in a mesh: section: 2 (over core), row: 4 (over y, x), col: 4 (over z).
Axes of the slice: x: 2, y: 2, z: 4, core: 2. Of those that a mesh axis runs over, the one named last changes fastest.
Arguments:
- inputs: float32 [2, 4096, 1024], P(None, 'row', 'col'), may hold values from -6 to 6
- out_grad: float32 [2, 4096, 1024], P(None, 'row', 'col'), may hold values from -6 to 6
- first_gain: float32 [2, 1024], P('section', 'col'), may hold values from 0.5 to 1.5
- first_shift: float32 [2, 1024], P('section', 'col'), may hold values from -3 to 3
- merged_weight: bfloat16 [2, 1024, 3, 1024], P('section', 'row', None, 'col'), may hold values from -0.1875 to 0.1875
- merged_bias: float32 [2, 2, 1024], P('section', None, 'col'), may hold values from -3 to 3
- proj_weight: bfloat16 [2, 1024, 1024], P('section', 'row', 'col'), may hold values from -1.5 to 1.5
- proj_bias: float32 [2, 1024], P('section', 'col'), may hold values from -3 to 3
- second_gain: float32 [2, 1024], P('section', 'col'), may hold values from 0.5 to 1.5
- second_shift: float32 [2, 1024], P('section', 'col'), may hold values from -3 to 3
- up_weight: bfloat16 [2, 1024, 4096], P('section', 'row', 'col'), may hold values from -0.1875 to 0.1875
- up_bias: float32 [2, 4096], P('section', 'col'), may hold values from -3 to 3
- down_weight: bfloat16 [2, 4096, 1024], P('section', 'col', 'row'), may hold values from -0.09375 to 0.09375
- down_bias: float32 [2, 1024], P('section', 'col'), may hold values from -3 to 3
Outputs:
- boundary: float32 [2, 2, 4096, 1024], P('section', None, 'row', 'col')
- first_gain_grad: float32 [2, 1024], P('section', 'col')
- first_shift_grad: float32 [2, 1024], P('section', 'col')
- merged_weight_grad: float32 [2, 1024, 3, 1024], P('section', 'row', None, 'col')
- merged_bias_grad: float32 [2, 2, 1024], P('section', None, 'col')
- proj_weight_grad: float32 [2, 1024, 1024], P('section', 'row', 'col')
- proj_bias_grad: float32 [2, 1024], P('section', 'col')
- second_gain_grad: float32 [2, 1024], P('section', 'col')
- second_shift_grad: float32 [2, 1024], P('section', 'col')
- up_weight_grad: float32 [2, 1024, 4096], P('section', 'row', 'col')
- up_bias_grad: float32 [2, 4096], P('section', 'col')
- down_weight_grad: float32 [2, 4096, 1024], P('section', 'col', 'row')
- down_bias_grad: float32 [2, 1024], P('section', 'col')
The draws below stay inside these ranges and needn't reach their ends.
All inputs are finite; a program needn't handle non-finite values.
Results may differ from the reference program's by a relative error of at most 0.017.
Values may be sent and summed in bfloat16 or wider, within the bound.
No kernel may reach another device: no remote copies, remote signals or barrier semaphores. Data moves between devices by JAX's collectives and lax.ppermute only.
A program may use at most 192 MiB of HBM per device.

```python
import jax
import jax.numpy as jnp
from jax import lax

D = 1024
HEADS = 16
HD = 64
FF = 4096
SEQ = 1024
MICRO = 2
ROWS = 4096
N_ROW = 4


def level_of(rng, dims, pieces, least, high):
    factor_of, own = 1.0, jax.random.fold_in(rng, 6)
    for dim, blocks in pieces:
        draws = jnp.exp(jax.random.uniform(jax.random.fold_in(own, dim), (blocks,), jnp.float32, least / len(pieces), high / len(pieces)))
        factor_of = factor_of * jnp.repeat(draws, dims[dim] // blocks).reshape([-1 if axis == dim else 1 for axis in range(len(dims))])
    return factor_of


def centred(rng, extent, width, most, split=(), kind=jnp.bfloat16):
    values = width * jax.random.normal(rng, extent, jnp.float32)
    if split:
        values = values * level_of(rng, extent, split, -0.22, 0.18)
    return jnp.clip(values, -most, most).astype(kind)


def setup_inputs(seed: int = 0) -> dict:
    seeds = jax.random.split(jax.random.key(seed), 15)
    inputs = centred(seeds[0], (MICRO, ROWS, D), 1.0, 6.0, ((1, 4), (2, 4)), jnp.float32)
    out_grad = centred(seeds[1], (MICRO, ROWS, D), 1.0, 6.0, ((1, 4), (2, 4)), jnp.float32)
    first_gain = jnp.clip(1.0 + 0.1 * jax.random.normal(seeds[2], (2, D), jnp.float32), 0.5, 1.5)
    first_shift = centred(seeds[3], (2, D), 0.5, 3.0, ((0, 2), (1, 4)), jnp.float32)
    merged_weight = centred(seeds[4], (2, D, 3, D), D ** -0.5, 0.1875, ((0, 2), (1, 4), (3, 4)))
    merged_bias = centred(seeds[5], (2, 2, D), 0.5, 3.0, ((0, 2), (2, 4)), jnp.float32)
    proj_weight = centred(seeds[6], (2, D, D), (D // 64) ** -0.5, 1.5, ((0, 2), (1, 4), (2, 4)))
    proj_bias = centred(seeds[7], (2, D), 0.5, 3.0, ((0, 2), (1, 4)), jnp.float32)
    second_gain = jnp.clip(1.0 + 0.1 * jax.random.normal(seeds[8], (2, D), jnp.float32), 0.5, 1.5)
    second_shift = centred(seeds[9], (2, D), 0.5, 3.0, ((0, 2), (1, 4)), jnp.float32)
    up_weight = centred(seeds[10], (2, D, FF), D ** -0.5, 0.1875, ((0, 2), (1, 4), (2, 4)))
    up_bias = centred(seeds[11], (2, FF), 0.5, 3.0, ((0, 2), (1, 4)), jnp.float32)
    down_weight = centred(seeds[12], (2, FF, D), FF ** -0.5, 0.09375, ((0, 2), (1, 4), (2, 4)))
    down_bias = centred(seeds[13], (2, D), 0.5, 3.0, ((0, 2), (1, 4)), jnp.float32)
    return {"inputs": inputs, "out_grad": out_grad, "first_gain": first_gain, "first_shift": first_shift, "merged_weight": merged_weight, "merged_bias": merged_bias, "proj_weight": proj_weight, "proj_bias": proj_bias, "second_gain": second_gain, "second_shift": second_shift, "up_weight": up_weight, "up_bias": up_bias, "down_weight": down_weight, "down_bias": down_bias}


@jax.custom_vjp
def low(v):
    return lax.optimization_barrier(v.astype(jnp.bfloat16)).astype(jnp.float32)

@jax.custom_vjp
def low_back(v):
    return v

def low_keep(v):
    return (low(v), None)

def low_pass(kept, grad):
    return (grad,)

def back_keep(v):
    return (v, None)

def back_low(kept, grad):
    return (low(grad),)
low.defvjp(low_keep, low_pass)
low_back.defvjp(back_keep, back_low)

def norm_rows(values, gain, shift):
    mean = lax.optimization_barrier(jnp.mean(values, axis=-1, keepdims=True))
    variance = lax.optimization_barrier(jnp.mean(values * values, axis=-1, keepdims=True)) - mean * mean
    return (values - mean) * lax.rsqrt(variance + 1e-05) * gain + shift

def attend(triple):
    query, keys, values = triple
    exact = lax.Precision.HIGHEST
    scores = jnp.einsum('qhd,khd->hqk', query, keys, precision=exact) * HD ** (-0.5)
    scores = low_back(scores)
    position = jnp.arange(SEQ)
    allowed = position[:, None] >= position[None, :]
    scores = jnp.where(allowed[None], scores, -1e+30)
    top = lax.optimization_barrier(jnp.max(scores, axis=-1, keepdims=True))
    weights = jnp.exp(scores - top)
    probs = weights / lax.optimization_barrier(jnp.sum(weights, axis=-1, keepdims=True))
    return jnp.einsum('hqk,khd->qhd', low(probs), values, precision=exact)

def layer(inputs, params):
    exact = lax.Precision.HIGHEST
    first_gain, first_shift, merged_weight, merged_bias, proj_weight, proj_bias, second_gain, second_shift, up_weight, up_bias, down_weight, down_bias = params
    count = inputs.shape[0]
    normed = low(norm_rows(inputs, first_gain, first_shift))
    merged = jnp.einsum('nte,ecf->ntcf', normed, merged_weight, precision=exact)
    bias = jnp.stack([merged_bias[0], jnp.zeros_like(merged_bias[0]), merged_bias[1]])
    merged = low_back(low(merged + bias))
    heads = merged.reshape(count, SEQ, 3, HEADS, HD)
    mixed = lax.map(jax.checkpoint(attend), (heads[:, :, 0], heads[:, :, 1], heads[:, :, 2]))
    mixed = low_back(low(mixed.reshape(count, SEQ, D)))
    branch = low_back(jnp.einsum('nte,ef->ntf', mixed, proj_weight, precision=exact) + proj_bias)
    middle = inputs + branch
    normed_two = low(norm_rows(middle, second_gain, second_shift))
    upper = low_back(jnp.einsum('nte,ef->ntf', normed_two, up_weight, precision=exact) + up_bias)
    active = low(jax.nn.gelu(upper, approximate=True))
    branch_two = low_back(jnp.einsum('ntf,fe->nte', active, down_weight, precision=exact) + down_bias)
    return middle + branch_two

def reference(inputs, out_grad, first_gain, first_shift, merged_weight, merged_bias, proj_weight, proj_bias, second_gain, second_shift, up_weight, up_bias, down_weight, down_bias):
    params = [first_gain, first_shift, merged_weight, merged_bias, proj_weight, proj_bias, second_gain, second_shift, up_weight, up_bias, down_weight, down_bias]
    params = [item.astype(jnp.float32) for item in params]
    starts = inputs.astype(jnp.float32).reshape(MICRO, N_ROW, SEQ, D)
    grads = out_grad.astype(jnp.float32).reshape(MICRO, N_ROW, SEQ, D)

    def whole(values, weights):
        first = [item[0] for item in weights]
        second = [item[1] for item in weights]
        link = low_back(low(layer(values, first)))
        return layer(link, second)

    def one_batch(totals, pair):
        values, grad = pair
        result, pull = jax.vjp(whole, values, params)
        back_in, back_params = pull(grad)
        totals = [left + right for left, right in zip(totals, back_params)]
        return (totals, (result, back_in))
    zeros = [jnp.zeros_like(item) for item in params]
    totals, (results, backs) = lax.scan(one_batch, zeros, (starts, grads))
    boundary = jnp.stack([backs.reshape(MICRO, N_ROW * SEQ, D), results.reshape(MICRO, N_ROW * SEQ, D)])
    return (boundary, totals[0], totals[1], totals[2], totals[3], totals[4], totals[5], totals[6], totals[7], totals[8], totals[9], totals[10], totals[11])
```

```python
import jax
import jax.numpy as jnp
from jax import lax
from jax.experimental import pallas as pl
from jax.experimental.pallas import tpu as pltpu
from jax.sharding import Mesh
from jax.sharding import PartitionSpec as P

D = 1024
HD = 64
EPS = 1e-05
SCALE = HD ** (-0.5)
BF = jnp.bfloat16
F32 = jnp.float32

TEAM = ("section", "peer")


def mm(a, b, ca=1, cb=0, out=F32):
    r = lax.dot_general(a, b, (((ca,), (cb,)), ((), ())), preferred_element_type=F32)
    return r.astype(out)


def swap_section(x):
    return lax.ppermute(x, "section", [(0, 1), (1, 0)])


def rotate_peer(x, by):
    n = lax.axis_size("peer")
    return lax.ppermute(x, "peer", [(i, (i + by) % n) for i in range(n)])


def cross(x, pairs):
    return lax.ppermute(x, ("section", "half"), pairs)


def team_gather(x):
    n = lax.axis_size("peer")
    s, o = lax.axis_index("section"), lax.axis_index("peer")
    held = [x] + [rotate_peer(x, k) for k in range(1, n)]
    other = [swap_section(v) for v in held]
    mine = [lax.select_n(o, *[held[(i - j) % n] for i in range(n)]) if n > 1 else held[0] for j in range(n)]
    yours = [lax.select_n(o, *[other[(i - j) % n] for i in range(n)]) if n > 1 else other[0] for j in range(n)]
    first = s == 0
    return [jnp.where(first, a, b) for a, b in zip(mine, yours)] + [
        jnp.where(first, b, a) for a, b in zip(mine, yours)
    ]


def team_scatter(p):
    n = lax.axis_size("peer")
    s, o = lax.axis_index("section"), lax.axis_index("peer")
    half = p.shape[1] // 2
    blk = half // n
    got = swap_section(lax.dynamic_slice_in_dim(p, (1 - s) * half, half, 1))
    q = lax.dynamic_slice_in_dim(p, s * half, half, 1).astype(F32) + got.astype(F32)
    total = lax.dynamic_slice_in_dim(q, o * blk, blk, 1)
    for k in range(1, n):
        part = lax.dynamic_slice_in_dim(q, ((o + k) % n) * blk, blk, 1).astype(BF)
        total = total + rotate_peer(part, k).astype(F32)
    return total


def team_sum(x):
    n = lax.axis_size("peer")
    y = x
    for k in range(1, n):
        y = y + rotate_peer(x, k)
    return y + swap_section(y)


def attention_forward_kernel(qb, nh, qkv_ref, o_ref, lse_ref):
    t, blk = o_ref.shape
    lane = lax.broadcasted_iota(jnp.int32, (1, blk), 1) // HD
    slot = lax.broadcasted_iota(jnp.int32, (1, 128), 1)
    below = lax.broadcasted_iota(jnp.int32, (qb, qb), 0) >= lax.broadcasted_iota(jnp.int32, (qb, qb), 1)
    for i in range(t // qb):
        rows = pl.ds(i * qb, qb)
        n = (i + 1) * qb
        q = qkv_ref[rows, 0:blk]
        k = qkv_ref[0:n, blk : 2 * blk]
        v = qkv_ref[0:n, 2 * blk : 3 * blk]
        out = jnp.zeros((qb, blk), F32)
        stats = jnp.zeros((qb, 128), F32)
        for h in range(nh):
            qh = jnp.where(lane == h, q, jnp.zeros_like(q))
            s = mm(qh, k, 1, 1) * SCALE
            tail = jnp.where(below, s[:, n - qb :], -1e30)
            s = jnp.concatenate([s[:, : n - qb], tail], axis=1) if i else tail
            top = jnp.max(s, axis=1, keepdims=True)
            e = jnp.exp(s - top)
            total = jnp.sum(e, axis=1, keepdims=True)
            p = (e * (1.0 / total)).astype(BF)
            out = jnp.where(lane == h, mm(p, v, 1, 0), out)
            stats = jnp.where(slot == h, top + jnp.log(total), stats)
        o_ref[rows, :] = out.astype(BF)
        lse_ref[rows, :] = stats


def attention_backward_kernel(qb, nh, qkv_ref, lse_ref, do_ref, g_ref, dk_ref, dv_ref):
    t, blk = do_ref.shape
    lane = lax.broadcasted_iota(jnp.int32, (1, blk), 1) // HD
    below = lax.broadcasted_iota(jnp.int32, (qb, qb), 0) >= lax.broadcasted_iota(jnp.int32, (qb, qb), 1)
    for i in reversed(range(t // qb)):
        rows = pl.ds(i * qb, qb)
        n = (i + 1) * qb
        q = qkv_ref[rows, 0:blk]
        k = qkv_ref[0:n, blk : 2 * blk]
        v = qkv_ref[0:n, 2 * blk : 3 * blk]
        do = do_ref[rows, :]
        dq = jnp.zeros((qb, blk), F32)
        dk = jnp.zeros((n, blk), F32)
        dv = jnp.zeros((n, blk), F32)
        for h in range(nh):
            mine = lane == h
            qh = jnp.where(mine, q, jnp.zeros_like(q))
            doh = jnp.where(mine, do, jnp.zeros_like(do))
            s = mm(qh, k, 1, 1) * SCALE
            tail = jnp.where(below, s[:, n - qb :], -1e30)
            s = jnp.concatenate([s[:, : n - qb], tail], axis=1) if i else tail
            p = jnp.exp(s - lse_ref[rows, h : h + 1])
            dp = mm(doh, v, 1, 1)
            delta = jnp.sum(p * dp, axis=1, keepdims=True)
            ds = (p * (dp - delta)).astype(BF)
            dq = jnp.where(mine, mm(ds, k, 1, 0), dq)
            dk = dk + mm(ds, qh, 0, 0)
            dv = dv + mm(p.astype(BF), doh, 0, 0)
        g_ref[rows, 0:blk] = (dq * SCALE).astype(BF)
        if n == t:
            dk_ref[...] = dk
            dv_ref[...] = dv
        else:
            dk_ref[0:n, :] += dk
            dv_ref[0:n, :] += dv
    g_ref[:, blk : 2 * blk] = (dk_ref[...] * SCALE).astype(BF)
    g_ref[:, 2 * blk : 3 * blk] = dv_ref[...].astype(BF)


def vmem(n):
    return [pl.BlockSpec(memory_space=pltpu.VMEM)] * n


def attention_forward(qkv):
    t, blk = qkv.shape[0], qkv.shape[1] // 3
    nh, qb = blk // HD, min(256, t)

    def body(*refs):
        attention_forward_kernel(qb, nh, *refs)

    return pl.pallas_call(
        body,
        out_shape=(jax.ShapeDtypeStruct((t, blk), BF), jax.ShapeDtypeStruct((t, 128), F32)),
        in_specs=vmem(1),
        out_specs=tuple(vmem(2)),
        cost_estimate=pl.CostEstimate(
            flops=4 * t * t * 256 * nh * 5 // 8, bytes_accessed=8 * t * blk, transcendentals=nh * t * t * 5 // 8
        ),
        name="attention_forward",
    )(qkv)


def attention_backward(qkv, lse, do):
    t, blk = do.shape
    nh, qb = blk // HD, min(256, t)

    def body(*refs):
        attention_backward_kernel(qb, nh, *refs)

    return pl.pallas_call(
        body,
        out_shape=jax.ShapeDtypeStruct((t, 3 * blk), BF),
        in_specs=vmem(3),
        out_specs=pl.BlockSpec(memory_space=pltpu.VMEM),
        scratch_shapes=[pltpu.VMEM((t, blk), F32), pltpu.VMEM((t, blk), F32)],
        cost_estimate=pl.CostEstimate(
            flops=10 * t * t * 256 * nh * 5 // 8, bytes_accessed=14 * t * blk, transcendentals=nh * t * t * 5 // 8
        ),
        name="attention_backward",
    )(qkv, lse, do)


def norm_gather(x, gain, shift):
    mean_own = jnp.mean(x, axis=1)
    moved = x - mean_own[:, None]
    blocks = team_gather(moved.astype(BF))
    sums = jnp.stack([jnp.sum(x, axis=1), jnp.sum(x * x, axis=1)])
    stats = team_gather(sums)
    total = sum(stats[1:], stats[0]) / D
    mean = total[0]
    inv = lax.rsqrt(total[1] - mean * mean + EPS)
    blk = x.shape[1]
    parts = [
        (b.astype(F32) + (st[0] / blk - mean)[:, None]) * inv[:, None] for b, st in zip(blocks, stats)
    ]
    normed = (jnp.concatenate(parts, axis=1) * gain + shift).astype(BF)
    return (x - mean[:, None]) * inv[:, None], inv, normed


def norm_back(partial, normed, gain, shift, centred, inv, gain_own):
    sums = jnp.stack(
        [
            jnp.sum(partial * gain, axis=1),
            jnp.sum(partial * (normed.astype(F32) - shift), axis=1),
        ]
    )
    sums = team_sum(sums) / D
    grad = team_scatter(partial.astype(BF))
    e = grad * gain_own
    back = inv[:, None] * (e - sums[0][:, None] - centred * sums[1][:, None])
    return grad, back


def gelu_parts(u):
    c = 0.7978845608028654
    th = jnp.tanh(c * (u + 0.044715 * u * u * u))
    act = 0.5 * u * (1.0 + th)
    slope = 0.5 * (1.0 + th) + 0.5 * u * (1.0 - th * th) * c * (1.0 + 3 * 0.044715 * u * u)
    return act, slope


def layer_forward(x, par, w):
    centred1, inv1, h1 = norm_gather(x, par["g1"], par["s1"])
    qkv = (mm(h1, w["merged"]) + par["mb"]).astype(BF)
    mixed_own, lse = attention_forward(qkv)
    mixed = jnp.concatenate(team_gather(mixed_own), axis=1)
    middle = x + mm(mixed, w["proj"]) + par["pb_own"]
    centred2, inv2, h2 = norm_gather(middle, par["g2"], par["s2"])
    upper = mm(h2, w["up"]) + par["ub"]
    active = gelu_parts(upper)[0].astype(BF)
    y = middle + team_scatter(mm(active, w["down"], 1, 1, BF)) + par["db_own"]
    return y, (centred1, inv1, h1, qkv, lse, mixed, centred2, inv2, h2, upper, active)


def layer_backward(g, par, w, kept):
    centred1, inv1, h1, qkv, lse, mixed, centred2, inv2, h2, upper, active = kept
    dy_own = g.astype(BF)
    small = {"db": jnp.sum(dy_own.astype(F32), axis=0)}
    large = {}
    dy = jnp.concatenate(team_gather(dy_own), axis=1)
    du = (mm(dy, w["down"]) * gelu_parts(upper)[1]).astype(BF)
    small["ub"] = jnp.sum(du.astype(F32), axis=0)
    dh2, back = norm_back(mm(du, w["up"], 1, 1), h2, par["g2"], par["s2"], centred2, inv2, par["g2_own"])
    large["down"] = mm(dy, active, 0, 0, BF)
    large["up"] = mm(h2, du, 0, 0, BF)
    small["g2"] = jnp.sum(dh2 * centred2, axis=0)
    small["s2"] = jnp.sum(dh2, axis=0)
    dmiddle = g + back
    dproj = dmiddle.astype(BF)
    small["pb"] = jnp.sum(dproj.astype(F32), axis=0)
    dmixed = team_scatter(mm(dproj, w["proj"], 1, 1, BF)).astype(BF)
    large["proj"] = mm(mixed, dproj, 0, 0, BF)
    dqkv = attention_backward(qkv, lse, dmixed)
    blk = dmixed.shape[1]
    small["mb"] = jnp.sum(dqkv.astype(F32), axis=0)
    dh1, back = norm_back(mm(dqkv, w["merged"], 1, 1), h1, par["g1"], par["s1"], centred1, inv1, par["g1_own"])
    large["merged"] = mm(h1, dqkv, 0, 0, BF)
    small["g1"] = jnp.sum(dh1 * centred1, axis=0)
    small["s1"] = jnp.sum(dh1, axis=0)
    return dmiddle + back, large, small


def fetch_weight(x, layer):
    near = cross(x, [(2 * layer, 0), (2 * layer + 1, 3)])
    far = cross(x, [(2 * layer, 1), (2 * layer + 1, 2)])
    keeper = lax.axis_index("section") == lax.axis_index("half")
    return jnp.where(keeper, near, far)


def return_weight(g, layer):
    if layer == 0:
        far = cross(g, [(1, 0), (2, 1)])
        near = cross(g, [(3, 1)])
    else:
        far = cross(g, [(2, 3), (1, 2)])
        near = cross(g, [(0, 2)])
    keeper = lax.axis_index("section") == lax.axis_index("half")
    return jnp.where(keeper, g, near).astype(F32) + far.astype(F32)


def on_device(
    inputs,
    out_grad,
    first_gain,
    first_shift,
    merged_weight,
    merged_bias,
    proj_weight,
    proj_bias,
    second_gain,
    second_shift,
    up_weight,
    up_bias,
    down_weight,
    down_bias,
):
    s, h, o = lax.axis_index("section"), lax.axis_index("half"), lax.axis_index("peer")
    peers = lax.axis_size("peer")
    keeper = s == h
    rows, seq, blk = inputs.shape[1], inputs.shape[1], inputs.shape[2]
    block = s * peers + o

    def gathered(shard):
        return lax.all_gather(shard, "row", axis=0, tiled=True)

    shards = {
        "merged": merged_weight[0].reshape(merged_weight.shape[1], -1),
        "proj": proj_weight[0],
        "up": up_weight[0],
        "down": down_weight[0].T,
    }
    weights = [
        {name: gathered(fetch_weight(shards[name], layer)) for name in ("merged", "proj", "up", "down")}
        for layer in range(2)
    ]

    names = ("g1", "s1", "pb", "g2", "s2", "db", "mb0", "mb1", "ub")
    values = (
        first_gain[0],
        first_shift[0],
        proj_bias[0],
        second_gain[0],
        second_shift[0],
        down_bias[0],
        merged_bias[0, 0],
        merged_bias[0, 1],
        up_bias[0],
    )
    packed = jnp.concatenate(values)
    every = lax.all_gather(packed, ("section", "half", "peer"), axis=0)
    every = every.reshape(2, 2 * peers, -1)
    params = []
    for layer in range(2):
        par, at = {}, 0
        for name, value in zip(names, values):
            full = every[layer, :, at : at + value.shape[0]]
            at += value.shape[0]
            par[name] = full.reshape(-1)
            par[name + "_own"] = lax.dynamic_index_in_dim(full, block, 0, keepdims=False)
        par["mb"] = jnp.concatenate([par["mb0_own"], jnp.zeros((blk,), F32), par["mb1_own"]])
        par["ub"] = par["ub_own"]
        params.append(par)

    swap = [(0, 0), (1, 2), (2, 1), (3, 3)]

    def placed(x):
        return cross(jnp.where(s == 0, x[0], x[1]), swap)

    x0 = placed(inputs)
    grad = placed(out_grad)
    y0, kept0 = layer_forward(x0, params[0], weights[0])
    x1 = y0.astype(BF).astype(F32)
    y1, kept1 = layer_forward(x1, params[1], weights[1])
    gx1, large1, small1 = layer_backward(grad, params[1], weights[1], kept1)
    g0 = gx1.astype(BF).astype(F32)
    gx0, large0, small0 = layer_backward(g0, params[0], weights[0], kept0)

    y1b, gxb = y1.astype(BF), gx0.astype(BF)
    ya, yb = cross(y1b, [(0, 2), (3, 3)]), cross(y1b, [(1, 2), (2, 3)])
    ga, gb = cross(gxb, [(0, 0), (3, 1)]), cross(gxb, [(1, 0), (2, 1)])
    a = jnp.where(s == 0, ga, ya).astype(F32)
    b = jnp.where(s == 0, gb, yb).astype(F32)
    boundary = jnp.where(h == 0, jnp.stack([a, b]), jnp.stack([b, a]))[None]

    def scattered(g, layer):
        return return_weight(lax.psum_scatter(g, "row", scatter_dimension=0, tiled=True), layer)

    grads = {}
    for name in ("down", "up", "proj", "merged"):
        one = scattered(large1[name], 1)
        zero = scattered(large0[name], 0)
        grads[name] = jnp.where(s == 0, zero, one)

    order = ("g1", "s1", "mb", "pb", "g2", "s2", "ub", "db")
    flat = [jnp.concatenate([sm[n] for n in order]) for sm in (small0, small1)]
    flat = lax.psum(jnp.stack(flat), ("row", "half"))
    got = swap_section(jnp.where(s == 0, flat[1], flat[0]))
    flat = jnp.where(keeper, jnp.where(s == 0, flat[0], flat[1]), got)
    small, at = {}, 0
    for n in order:
        size = small0[n].shape[0]
        small[n] = flat[at : at + size]
        at += size
    mb = small["mb"].reshape(3, blk)
    return (
        boundary,
        small["g1"][None],
        small["s1"][None],
        grads["merged"].reshape(merged_weight.shape),
        jnp.stack([mb[0], mb[2]])[None],
        grads["proj"][None],
        small["pb"][None],
        small["g2"][None],
        small["s2"][None],
        grads["up"][None],
        small["ub"][None],
        grads["down"].T[None],
        small["db"][None],
    )


def solution(mesh):
    sizes = mesh.shape
    col = ("half", "peer")
    team_mesh = Mesh(
        mesh.devices.reshape(sizes["section"], sizes["row"], 2, sizes["col"] // 2),
        ("section", "row", "half", "peer"),
    )
    placed = (
        P(None, "row", col),
        P(None, "row", col),
        P("section", col),
        P("section", col),
        P("section", "row", None, col),
        P("section", None, col),
        P("section", "row", col),
        P("section", col),
        P("section", col),
        P("section", col),
        P("section", "row", col),
        P("section", col),
        P("section", col, "row"),
        P("section", col),
    )
    return jax.shard_map(
        on_device,
        mesh=team_mesh,
        in_specs=placed,
        out_specs=(
            P("section", None, "row", col),
            P("section", col),
            P("section", col),
            P("section", "row", None, col),
            P("section", None, col),
            P("section", "row", col),
            P("section", col),
            P("section", col),
            P("section", col),
            P("section", "row", col),
            P("section", col),
            P("section", col, "row"),
            P("section", col),
        ),
        check_vma=False,
    )
```
